32 devices in a mesh: gx: 4 (over y, x), gy: 4 (over z), gz: 2 (over core).
Axes of the slice: x: 2, y: 2, z: 4, core: 2. Of those that a mesh axis runs over, the one named last changes fastest.
Arguments:
- coords: float32 [4, 4, 6, 3, 128], P('gx', 'gy', 'gz'), as said below
- polar: float32 [4, 4, 6, 128], P('gx', 'gy', 'gz'), may hold values from 0.3 to 1.2
- field: float32 [4, 4, 6, 6, 128], P('gx', 'gy', 'gz'), may hold values from -6 to 6
- atom_count: int32 [4, 4, 6], P('gx', 'gy', 'gz'), may hold values from 64 to 128, as said below
- pair_list: int32 [4, 4, 6, 13], P('gx', 'gy', 'gz'), may hold values from -1 to 26, as said below
Outputs:
- dipoles: float32 [4, 4, 6, 6, 128], P('gx', 'gy', 'gz')
- residual: float32 [4, 4, 6, 6, 128], P('gx', 'gy', 'gz')
The draws below stay inside these ranges and needn't reach their ends.
Inputs may be any that keep to these rules, and one draw needn't show every extreme that they name: `coords`: each coordinate lies within a quarter of 2.2 of its lattice site: atom slot a sits at 2.2 (a % 4 + 0.5, (a // 4) % 4 + 0.5, a // 16 + 0.5). `atom_count`: some block holds 128 atoms. `pair_list`: each block's row holds distinct codes above 13 in ascending order, followed by -1 in the unused entries.
All inputs are finite; a program needn't handle non-finite values.
Results may differ from the reference program's by a relative error of at most 0.0003.
Values sent between devices are 32-bit elements; how exact they have to be, the bound alone decides.
A program may use at most 64 MiB of HBM per device.

```python
import math
import jax
import jax.numpy as jnp
from jax import lax

ATOMS = 128
ITERS = 2
NBX = 4
NBY = 4
NBZ = 6


spacing = 2.2


def draw_coords(key, part):
    lattice_ids = jnp.arange(ATOMS, dtype=jnp.int32)
    lattice = jnp.stack([lattice_ids % 4, lattice_ids // 4 % 4, lattice_ids // 16]).astype(jnp.float32)
    lattice_pos = (lattice + 0.5) * spacing
    jitter = jax.random.uniform(key, (NBX, NBY, NBZ, 3, ATOMS), jnp.float32, -0.2, 0.2)
    return (lattice_pos + jitter * spacing).astype(jnp.float32)


def draw_atom_count(key, part):
    counts = jax.random.randint(key, (NBX, NBY, NBZ), ATOMS // 2, ATOMS + 1)
    return counts.at[0, 0, 0].set(ATOMS).astype(jnp.int32)


def draw_pair_list(key, part):
    dice_rolls = jax.random.randint(key, (NBX, NBY, NBZ, 13), 0, 100)
    density = jnp.arange(NBX, dtype=jnp.int32) * 60 // NBX + 30
    chosen = dice_rolls < density[:, None, None, None]
    forward_codes = jnp.arange(14, 27, dtype=jnp.int32)
    sort_keys = jnp.where(chosen, forward_codes, forward_codes + 100)
    ordered = jnp.sort(sort_keys, axis=-1)
    return jnp.where(ordered < 100, ordered, -1).astype(jnp.int32)


def shard_levels(stream_key, extent, pieces, least, top_value):
    def one(position, parts):
        draws = jax.random.uniform(jax.random.fold_in(jax.random.fold_in(stream_key, 6), position), (parts,), jnp.float32, least / len(pieces), top_value / len(pieces))
        return jnp.repeat(jnp.exp(draws), extent[position] // parts).reshape((-1,) + (1,) * (len(extent) - position - 1))

    gain = one(*pieces[0])
    for cut in pieces[1:]:
        gain = gain * one(*cut)
    return gain


def noise(rng, shape, scale, bound, split=(), held_as=jnp.bfloat16):
    result = jax.random.normal(rng, shape, jnp.float32) * scale
    if len(split) > 0:
        result = shard_levels(rng, shape, split, -0.22, 0.18) * result
    return jnp.clip(result, min=-bound, max=bound).astype(held_as)


def setup_inputs(seed: int = 0) -> dict:
    seeds = jax.random.split(jax.random.key(seed), 6)
    return {
        "coords": draw_coords(jax.random.fold_in(seeds[5], 71), 0),
        "polar": jnp.clip(jnp.exp(math.log(1.2) - 1.3862944 * jax.random.uniform(seeds[1], (NBX, NBY, NBZ, ATOMS), jnp.float32) ** shard_levels(seeds[1], (NBX, NBY, NBZ, ATOMS), ((0, 4), (1, 4), (2, 2)), -0.2, 0.2)), 0.3, 1.2),
        "field": noise(seeds[2], (NBX, NBY, NBZ, 6, ATOMS), 1.0, 6.0, ((0, 4), (1, 4), (2, 2)), jnp.float32),
        "atom_count": draw_atom_count(jax.random.fold_in(seeds[5], 71), 0),
        "pair_list": draw_pair_list(jax.random.fold_in(seeds[5], 71), 0),
    }


spacing = 2.2
cutoff_square = 49.0
thole = 0.39
highest = lax.Precision.HIGHEST

def pair_weights(geometry_row, geometry_col, offset_vec, self_flag):
    separation = offset_vec[:, None, None] + geometry_col[0:3][:, None, :] - geometry_row[0:3][:, :, None]
    range_square = lax.optimization_barrier(jnp.sum(separation * separation, axis=0))
    diagonal = self_flag * jnp.eye(geometry_row.shape[1], dtype=jnp.float32)
    weight_mask = geometry_row[4][:, None] * geometry_col[4][None, :] * (1.0 - diagonal)
    range_square = range_square + diagonal
    inverse_range = lax.rsqrt(range_square)
    inverse_cube = inverse_range * inverse_range * inverse_range
    damp_argument = thole * range_square * jnp.sqrt(range_square) * lax.rsqrt(geometry_row[3][:, None] * geometry_col[3][None, :])
    damping = jnp.exp(-damp_argument)
    lam_three = 1.0 - damping
    lam_five = 1.0 - (1.0 + damp_argument) * damping
    switch = jnp.square(jnp.maximum(1.0 - range_square / cutoff_square, 0.0))
    weight_three = weight_mask * switch * lam_three * inverse_cube
    weight_five = 3.0 * weight_mask * switch * lam_five * inverse_cube * inverse_range * inverse_range
    return (weight_three, weight_five, separation)

def field_rows(weight_three, weight_five, separation, dipole_col):
    dipole_sets = dipole_col.reshape(2, 3, -1)
    projected = jnp.einsum('cij,scj->sij', separation, dipole_sets, precision=highest)
    radial = jnp.einsum('ij,cij,sij->sci', weight_five, separation, projected, precision=highest)
    direct = jnp.einsum('ij,scj->sci', weight_three, dipole_sets, precision=highest)
    return (radial - direct).reshape(6, -1)

def block_fields(geometry, neighbour_geo, neighbour_dip, active, offset_vec, self_flag):

    def slab_fields(inputs):
        geo_slab, near_geo, near_dip, act_slab = inputs
        atom_slots = geo_slab.shape[-1]

        def single_pair(geometry_row, geometry_col, dipole_col, switch_on):
            weight_three, weight_five, separation = pair_weights(geometry_row, geometry_col, offset_vec, self_flag)
            return switch_on * field_rows(weight_three, weight_five, separation, dipole_col)
        fields = jax.vmap(single_pair)(geo_slab.reshape(-1, 5, atom_slots), near_geo.reshape(-1, 5, atom_slots), near_dip.reshape(-1, 6, atom_slots), act_slab.reshape(-1))
        return fields.reshape(geo_slab.shape[0:2] + (6, atom_slots))
    return lax.map(slab_fields, (geometry, neighbour_geo, neighbour_dip, active))

def apply_operator(vector, geometry, forward, box_size):
    accumulated = jnp.zeros_like(vector)
    for pair_code in range(27):
        roll_by = (1 - pair_code // 9, 1 - pair_code // 3 % 3, 1 - pair_code % 3)
        neighbour_geo = jnp.roll(geometry, roll_by, axis=(0, 1, 2))
        neighbour_dip = jnp.roll(vector, roll_by, axis=(0, 1, 2))
        if pair_code == 13:
            active = jnp.ones(forward.shape[0:3], jnp.float32)
        elif pair_code > 13:
            active = forward[..., pair_code]
        else:
            active = jnp.roll(forward[..., 26 - pair_code], roll_by, axis=(0, 1, 2))
        offset_vec = box_size * jnp.array([pair_code // 9 - 1, pair_code // 3 % 3 - 1, pair_code % 3 - 1], jnp.float32)
        self_flag = 1.0 if pair_code == 13 else 0.0
        accumulated = accumulated + block_fields(geometry, neighbour_geo, neighbour_dip, active, offset_vec, self_flag)
    return vector / geometry[:, :, :, 3:4, :] - accumulated

def set_sums(former, latter):
    product = (former * latter).reshape(former.shape[0:3] + (2, 3, former.shape[-1]))
    return lax.optimization_barrier(jnp.sum(product, axis=(0, 1, 2, 4, 5)))

def spread(values):
    return jnp.repeat(values, 3)[:, None]

def reference(coords, polar, field, atom_count, pair_list):
    atom_slots = coords.shape[-1]
    slot_ids = jnp.arange(atom_slots, dtype=jnp.int32)
    atom_mask = (slot_ids[None, None, None, :] < atom_count[..., None]).astype(jnp.float32)
    geometry = jnp.concatenate([coords, polar[..., None, :], atom_mask[..., None, :]], axis=3)
    pair_codes = jnp.arange(27, dtype=jnp.int32)
    forward = jnp.any(pair_list[..., :, None] == pair_codes, axis=-2).astype(jnp.float32)
    box_size = jnp.array([4.0 * spacing, 4.0 * spacing, spacing * (atom_slots // 16)], jnp.float32)
    polar_col = geometry[:, :, :, 3:4, :]
    source = field * atom_mask[..., None, :]
    dipoles = polar_col * source
    residual = source - apply_operator(dipoles, geometry, forward, box_size)
    precond = polar_col * residual
    direction = precond
    norm_now = set_sums(residual, precond)
    for iteration in range(ITERS):
        operated = apply_operator(direction, geometry, forward, box_size)
        step_len = spread(norm_now / set_sums(direction, operated))
        dipoles = dipoles + step_len * direction
        residual = residual - step_len * operated
        if iteration + 1 < ITERS:
            precond = polar_col * residual
            norm_next = set_sums(residual, precond)
            direction = precond + spread(norm_next / norm_now) * direction
            norm_now = norm_next
    return (dipoles, residual)
```

```python
import functools

import jax
import jax.numpy as jnp
from jax import lax
from jax.experimental import pallas as pl
from jax.experimental.pallas import tpu as pltpu
from jax.sharding import PartitionSpec as P

ITERS = 2


spacing = 2.2
cutoff_square = 49.0
thole = 0.39
chunk = 16


def extended(cells, sides, width):
    for axis, dim in sides:
        count = lax.axis_size(axis)
        head = lax.slice_in_dim(cells, 0, width, axis=dim)
        tail = lax.slice_in_dim(cells, cells.shape[dim] - width, cells.shape[dim], axis=dim)
        cells = jnp.concatenate(
            [
                lax.ppermute(tail, axis, [(i, (i + 1) % count) for i in range(count)]),
                cells,
                lax.ppermute(head, axis, [((i + 1) % count, i) for i in range(count)]),
            ],
            axis=dim,
        )
    return cells


def operator_kernel(blocks, box_size, flags_ref, geo_ref, vec_ref, out_ref, own_ref, acc_ref):
    block_x, block_y, block_z = blocks
    ext_y, ext_z = block_y + 2, block_z + 2
    slots = geo_ref.shape[-1]
    ones = jnp.ones((8, slots), jnp.float32)

    def pair(near, offset, is_self):
        rows = geo_ref[near]
        near_x = rows[0:1] + offset[0]
        near_y = rows[1:2] + offset[1]
        near_z = rows[2:3] + offset[2]
        near_p = thole * lax.rsqrt(rows[3:4])
        vec = vec_ref[near] * rows[4:5]
        for start in range(0, slots, chunk):
            span = pl.ds(start, chunk)
            dx = near_x - own_ref[0, span, :]
            dy = near_y - own_ref[1, span, :]
            dz = near_z - own_ref[2, span, :]
            square = dx * dx + dy * dy + dz * dz
            if is_self:
                row_id = lax.broadcasted_iota(jnp.int32, (chunk, slots), 0) + start
                col_id = lax.broadcasted_iota(jnp.int32, (chunk, slots), 1)
                same = row_id == col_id
                square = jnp.where(same, 1.0, square)
            inverse = lax.rsqrt(square)
            inverse_square = inverse * inverse
            damp = square * square * inverse * (near_p * own_ref[3, span, :])
            damping = jnp.exp(-damp)
            switch = jnp.maximum(1.0 - square * (1.0 / cutoff_square), 0.0)
            scale = switch * switch * (inverse_square * inverse)
            weight_three = scale * (1.0 - damping)
            weight_five = (1.0 - (1.0 + damp) * damping) * scale * (3.0 * inverse_square)
            if is_self:
                weight_three = jnp.where(same, 0.0, weight_three)
                weight_five = jnp.where(same, 0.0, weight_five)
            for dipole_set in range(2):
                vx = vec[3 * dipole_set : 3 * dipole_set + 1]
                vy = vec[3 * dipole_set + 1 : 3 * dipole_set + 2]
                vz = vec[3 * dipole_set + 2 : 3 * dipole_set + 3]
                along = (dx * vx + dy * vy + dz * vz) * weight_five
                acc_ref[3 * dipole_set, span, :] += dx * along - weight_three * vx
                acc_ref[3 * dipole_set + 1, span, :] += dy * along - weight_three * vy
                acc_ref[3 * dipole_set + 2, span, :] += dz * along - weight_three * vz

    @pl.loop(0, block_x * block_y * block_z)
    def _(block_id):
        place_x = block_id // (block_y * block_z) + 1
        place_y = block_id // block_z % block_y + 1
        place_z = block_id % block_z + 1
        own = (place_x * ext_y + place_y) * ext_z + place_z
        rows = geo_ref[own]
        for part in range(4):
            row = rows[part : part + 1]
            if part == 3:
                row = lax.rsqrt(row)
            own_ref[part] = jnp.broadcast_to(row, (slots, slots)).T
        acc_ref[...] = jnp.zeros_like(acc_ref)
        pair(own, (0.0, 0.0, 0.0), True)

        @pl.loop(0, 27)
        def _(code):
            off_x, off_y, off_z = code // 9 - 1, code // 3 % 3 - 1, code % 3 - 1
            near = own + (off_x * ext_y + off_y) * ext_z + off_z
            forward = flags_ref[own, code]
            backward = flags_ref[near, 26 - code]
            active = jnp.where(code > 13, forward, jnp.where(code < 13, backward, 0))

            @pl.when(active > 0)
            def _():
                offset = (
                    off_x.astype(jnp.float32) * box_size[0],
                    off_y.astype(jnp.float32) * box_size[1],
                    off_z.astype(jnp.float32) * box_size[2],
                )
                pair(near, offset, False)

        mask = rows[4:5]
        polar = rows[3:4]
        for part in range(6):
            total = lax.dot_general(
                ones,
                acc_ref[part],
                (((1,), (1,)), ((), ())),
                precision=lax.Precision.HIGHEST,
                preferred_element_type=jnp.float32,
            )
            vec_row = vec_ref[own, pl.ds(part, 1), :]
            out_ref[block_id, pl.ds(part, 1), :] = vec_row / polar - mask * total[0:1]


def set_sums(former, latter):
    product = (former * latter).reshape(former.shape[0:3] + (2, 3, former.shape[-1]))
    return jnp.sum(product, axis=(0, 1, 2, 4, 5))


def spread(values):
    return jnp.repeat(values, 3)[:, None]


def global_pair(residual, precond, operated):
    both = jnp.concatenate([set_sums(residual, precond), set_sums(precond, operated)])
    both = lax.psum(both, ("gx", "gy", "gz"))
    return both[0:2], both[2:4]


def on_device(coords, polar, field, atom_count, pair_list):
    blocks = coords.shape[0:3]
    block_x, block_y, block_z = blocks
    slots = coords.shape[-1]
    sides = (("gz", 2), ("gy", 1), ("gx", 0))
    slot_ids = jnp.arange(slots, dtype=jnp.int32)
    atom_mask = (slot_ids < atom_count[..., None]).astype(jnp.float32)[..., None, :]
    forward = jnp.any(pair_list[..., :, None] == slot_ids, axis=-2).astype(jnp.float32)
    polar_col = polar[..., None, :]
    source = field * atom_mask
    dipoles = polar_col * source
    packed = jnp.concatenate(
        [coords, polar_col, atom_mask, dipoles, forward[..., None, :]], axis=3
    )
    packed_ext = extended(packed, sides, 1).reshape(-1, 12, slots)
    flags = packed_ext[:, 11, :].astype(jnp.int32)
    geo_ext = packed_ext[:, 0:8]
    box_size = (4.0 * spacing, 4.0 * spacing, spacing * (slots // 16))
    total = block_x * block_y * block_z
    vmem = pl.BlockSpec(memory_space=pltpu.VMEM)
    apply_kernel = pl.pallas_call(
        functools.partial(operator_kernel, blocks, box_size),
        out_shape=jax.ShapeDtypeStruct((total, 6, slots), jnp.float32),
        in_specs=[pl.BlockSpec(memory_space=pltpu.SMEM), vmem, vmem],
        out_specs=vmem,
        scratch_shapes=[
            pltpu.VMEM((4, slots, slots), jnp.float32),
            pltpu.VMEM((6, slots, slots), jnp.float32),
        ],
    )

    def operator_ext(vector_ext):
        return apply_kernel(flags, geo_ext, vector_ext).reshape(dipoles.shape)

    def operator(vector):
        return operator_ext(extended(vector, sides, 1).reshape(-1, 6, slots))

    residual = source - operator_ext(packed_ext[:, 5:11])
    precond = polar_col * residual
    operated = operator(precond)
    norm_now, curve = global_pair(residual, precond, operated)
    step_len = norm_now / curve
    direction = precond
    projected = operated
    for iteration in range(ITERS):
        dipoles = dipoles + spread(step_len) * direction
        residual = residual - spread(step_len) * projected
        if iteration + 1 < ITERS:
            precond = polar_col * residual
            operated = operator(precond)
            norm_next, curve = global_pair(residual, precond, operated)
            conj_ratio = norm_next / norm_now
            step_len = norm_next / (curve - conj_ratio * norm_next / step_len)
            direction = precond + spread(conj_ratio) * direction
            projected = operated + spread(conj_ratio) * projected
            norm_now = norm_next
    return (dipoles, residual)


def solution(mesh):
    return jax.shard_map(
        on_device,
        mesh=mesh,
        in_specs=(
            P("gx", "gy", "gz", None, None),
            P("gx", "gy", "gz", None),
            P("gx", "gy", "gz", None, None),
            P("gx", "gy", "gz"),
            P("gx", "gy", "gz", None),
        ),
        out_specs=(P("gx", "gy", "gz", None, None), P("gx", "gy", "gz", None, None)),
        check_vma=False,
    )
```
